32 devices in a mesh: grp: 4 (over y, x), pos: 8 (over z, core).
Axes of the slice: x: 2, y: 2, z: 4, core: 2. Of those that a mesh axis runs over, the one named last changes fastest.
Arguments:
- tiles: float32 [4, 8, 12, 256, 256], P('grp', 'pos'), may hold values from -0.109375 to 0.109375
- tile_row: int32 [4, 8, 12], P('grp', 'pos'), may hold values from 0 to 7
- tile_col: int32 [4, 8, 12], P('grp', 'pos'), may hold values from 0 to 7
- tile_count: int32 [4, 8], P('grp', 'pos'), may hold values from 1 to 12, as said below
- energies: float32 [16384], P('pos'), may hold values from 1 to 10
- basis: float32 [16, 16384], P(None, 'pos'), may hold values from -6 to 6
- prev_basis: float32 [16, 16384], P(None, 'pos'), may hold values from -6 to 6
- beta_prev: float32 [16, 16], replicated, may hold values from -3 to 3
Outputs:
- next_basis: float32 [16, 16384], P(None, 'pos')
- alpha: float32 [16, 16], replicated
- beta: float32 [16, 16], replicated
The draws below stay inside these ranges and needn't reach their ends.
Inputs may be any that keep to these rules, and one draw needn't show every extreme that they name: `tile_count`: some segment of some diagonal uses all 12 slots in every draw.
All inputs are finite; a program needn't handle non-finite values.
Results may differ from the reference program's by a relative error of at most 0.00021.
Values sent between devices are 32-bit elements; how exact they have to be, the bound alone decides.
A program may use at most 64 MiB of HBM per device.

```python
import math
import jax
import jax.numpy as jnp
from jax import lax

TILE = 256
BLOCK = 16
TPS = 8
MAXT = 12
GROUPS = 4
SEGS = 8
NDIM = 16384


def draw_tile_count(key, part):
    first_key, second_key = jax.random.split(jax.random.fold_in(key, 17))
    counts = jax.random.randint(first_key, (GROUPS * SEGS,), 1, MAXT + 1)
    chosen = jax.random.randint(second_key, (), 0, GROUPS * SEGS)
    counts = counts.at[chosen].set(MAXT)
    return counts.reshape(GROUPS, SEGS).astype(jnp.int32)


def with_ends(drawn, rng, least, largest):
    shape = drawn.shape
    index_at = [jax.random.randint(jax.random.fold_in(rng, axis), (), 0, shape[axis]) for axis in range(len(shape))]
    drawn = drawn.at[tuple(index_at)].set(least)
    longest = shape.index(max(shape))
    index_at[longest] = (index_at[longest] + 1) % shape[longest]
    return drawn.at[tuple(index_at)].set(largest)


def steps_of(own_key, extent, pieces, least, high):
    def one(position, blocks):
        steps = jax.random.uniform(jax.random.fold_in(jax.random.fold_in(own_key, 6), position), (blocks,), jnp.float32, least / len(pieces), high / len(pieces))
        return jnp.repeat(jnp.exp(steps), extent[position] // blocks).reshape((-1,) + (1,) * (len(extent) - position - 1))

    gain = one(*pieces[0])
    for cut in pieces[1:]:
        gain = gain * one(*cut)
    return gain


def bell_draw(key, dims, deviation, most, shards=(), kind=jnp.bfloat16):
    entries = deviation * jax.random.normal(key, dims, jnp.float32)
    if shards:
        entries = entries * steps_of(key, dims, shards, -0.22, 0.18)
    return jnp.clip(entries, -most, most).astype(kind)


def setup_inputs(seed: int = 0) -> dict:
    key_of = jax.random.split(jax.random.key(seed), 9)
    tiles = bell_draw(key_of[0], (GROUPS, SEGS, MAXT, TILE, TILE), (2 * TILE * MAXT * GROUPS // TPS) ** -0.5, 0.109375, ((0, 4), (1, 8)), jnp.float32)
    tile_row = with_ends(jax.random.randint(key_of[1], (GROUPS, SEGS, MAXT), 0, TPS), jax.random.fold_in(key_of[1], 1), 0, TPS - 1).astype(jnp.int32)
    tile_col = with_ends(jax.random.randint(key_of[2], (GROUPS, SEGS, MAXT), 0, TPS), jax.random.fold_in(key_of[2], 1), 0, TPS - 1).astype(jnp.int32)
    tile_count = draw_tile_count(jax.random.fold_in(key_of[8], 71), 0)
    energies = jnp.clip(jnp.exp(math.log(10.0) - 2.3025851 * jax.random.uniform(key_of[4], (NDIM,), jnp.float32) ** steps_of(key_of[4], (NDIM,), ((0, 8),), -0.2, 0.2)), 1.0, 10.0)
    basis = bell_draw(key_of[5], (BLOCK, NDIM), 1.0, 6.0, ((1, 8),), jnp.float32)
    prev_basis = bell_draw(key_of[6], (BLOCK, NDIM), 1.0, 6.0, ((1, 8),), jnp.float32)
    beta_prev = bell_draw(key_of[7], (BLOCK, BLOCK), 0.5, 3.0, (), jnp.float32)
    return {"tiles": tiles, "tile_row": tile_row, "tile_col": tile_col, "tile_count": tile_count, "energies": energies, "basis": basis, "prev_basis": prev_basis, "beta_prev": beta_prev}


def matmul(left, right):
    return jnp.dot(left, right, precision=lax.Precision.HIGHEST)

def reference(tiles, tile_row, tile_col, tile_count, energies, basis, prev_basis, beta_prev):
    group_ids = jnp.arange(GROUPS, dtype=jnp.int32)[:, None, None]
    pos_ids = jnp.arange(SEGS, dtype=jnp.int32)[None, :, None]
    slot_ids = jnp.arange(MAXT, dtype=jnp.int32)[None, None, :]
    row_start = ((pos_ids * TPS + tile_row) * TILE).astype(jnp.int32).reshape(-1)
    col_start = (((pos_ids + group_ids) % SEGS * TPS + tile_col) * TILE).astype(jnp.int32).reshape(-1)
    weight_on = (slot_ids < tile_count[:, :, None]).astype(jnp.float32).reshape(-1)
    block_data = tiles.reshape(-1, TILE, TILE)

    def advance(accumulated, entry):
        data, row_at, col_at, scale = entry
        from_col = lax.dynamic_slice_in_dim(basis, col_at, TILE, 1)
        from_row = lax.dynamic_slice_in_dim(basis, row_at, TILE, 1)
        to_row = matmul(from_col, data.T) * scale
        to_col = matmul(from_row, data) * scale
        current = lax.dynamic_slice_in_dim(accumulated, row_at, TILE, 1)
        accumulated = lax.dynamic_update_slice_in_dim(accumulated, current + to_row, row_at, 1)
        current = lax.dynamic_slice_in_dim(accumulated, col_at, TILE, 1)
        accumulated = lax.dynamic_update_slice_in_dim(accumulated, current + to_col, col_at, 1)
        return (accumulated, None)
    applied, unused = lax.scan(advance, jnp.zeros_like(basis), (block_data, row_start, col_start, weight_on))
    applied = applied + energies[None, :] * basis
    alpha = matmul(basis, applied.T) / NDIM
    residual = applied - matmul(alpha.T, basis) - matmul(beta_prev, prev_basis)
    gram = matmul(residual, residual.T) / NDIM
    factor = jnp.linalg.cholesky(gram)
    next_rows = jax.scipy.linalg.solve_triangular(factor, residual, lower=True)
    return (next_rows, alpha, factor)
```

```python
import functools

import jax
import jax.numpy as jnp
from jax import lax
from jax.experimental import pallas as pl
from jax.experimental.pallas import tpu as pltpu
from jax.sharding import PartitionSpec as P

MESH = pl.DeviceIdType.MESH
NT = (((1,), (1,)), ((), ()))
NN = (((1,), (0,)), ((), ()))
f32 = jnp.float32
bf16 = jnp.bfloat16


def exact(left, right, dims):
    return lax.dot_general(
        left, right, dims, precision=lax.Precision.HIGHEST, preferred_element_type=f32
    )


def split(values):
    high = values.astype(bf16)
    return high, (values - high.astype(f32)).astype(bf16)


def factored(gram):
    n = gram.shape[0]
    wide = jnp.concatenate([gram, jnp.eye(n, dtype=f32)], axis=1)
    row_at = lax.broadcasted_iota(jnp.int32, (n, 1), 0)
    done = jnp.zeros((n, 2 * n), f32)
    for j in range(n):
        column = wide[:, j : j + 1]
        scale = lax.rsqrt(wide[j : j + 1, j : j + 1])
        pivot = wide[j : j + 1, :] * scale
        done = jnp.where(row_at == j, pivot, done)
        wide = wide - jnp.where(row_at > j, column * scale, 0.0) * pivot
    return done[:, :n], done[:, n:]


def kernel(
    groups, segs,
    tiles_hbm, row_hbm, col_hbm, count_hbm, energies_hbm, basis_hbm, prev_hbm, beta_prev_hbm,
    next_ref, alpha_ref, beta_ref,
    tiles, rows, cols, count, energies, own, far, prev, beta_prev,
    own_split, far_split, products, back, forth, arrived, gathered, offset, both, early, late,
    in_sem, tile_sem, far_sem, back_send, back_recv, forth_send, forth_recv,
    gather_send, gather_recv, early_send, early_recv, late_send, late_recv,
):
    g, p = lax.axis_index("grp"), lax.axis_index("pos")
    slots, width = tiles.shape[0], tiles.shape[-1]
    vectors, length = own.shape
    sides = length // width
    part = length // groups
    total = float(length * segs)

    def at(group, pos):
        return (lax.rem(group + groups, groups), lax.rem(pos + segs, segs))

    def send(src, dst, send_sem, recv_sem, to):
        return pltpu.make_async_remote_copy(
            src_ref=src, dst_ref=dst, send_sem=send_sem, recv_sem=recv_sem,
            device_id=to, device_id_type=MESH,
        )

    small = [
        pltpu.make_async_copy(src, dst, in_sem.at[i])
        for i, (src, dst) in enumerate([
            (basis_hbm, own), (prev_hbm, prev), (energies_hbm, energies),
            (beta_prev_hbm, beta_prev), (row_hbm, rows), (col_hbm, cols), (count_hbm, count),
        ])
    ]
    for copy in small:
        copy.start()

    def tile_copy(k):
        return pltpu.make_async_copy(tiles_hbm.at[k], tiles.at[k], tile_sem.at[k])

    for k in range(slots):
        tile_copy(k).start()

    barrier = pltpu.get_barrier_semaphore()
    greeted = 0
    for d in range(1, segs):
        pl.semaphore_signal(barrier, inc=1, device_id=at(g, p + d), device_id_type=MESH)
        greeted += 1
    for d in range(1, groups):
        pl.semaphore_signal(barrier, inc=1, device_id=at(g + d, p), device_id_type=MESH)
        source = lax.rem(g - d + groups, groups)
        pl.semaphore_signal(barrier, inc=1, device_id=at(source, p - source), device_id_type=MESH)
        greeted += 2

    for copy in small:
        copy.wait()

    def stack(ref, out):
        for t in range(sides):
            high, low = split(ref[:, t * width : (t + 1) * width])
            out[t] = jnp.concatenate([high, low], axis=0)

    def multiply(picked, k, dims):
        high, low = split(tiles[k])
        both_parts = lax.dot_general(picked, high, dims, preferred_element_type=f32)
        both_parts += lax.dot_general(picked, low, dims, preferred_element_type=f32)
        return both_parts[:vectors] + both_parts[vectors:]

    def scatter(index, out):
        for t in range(sides):
            value = jnp.zeros((vectors, width), f32)
            for k in range(slots):
                live = jnp.logical_and(index[0, k] == t, k < count[0, 0])
                value = value + products[k] * jnp.where(live, 1.0, 0.0).astype(f32)
            step = min(width, part)
            for c in range(0, width, step):
                lane = t * width + c
                out[lane // part, :, lane % part : lane % part + step] = value[:, c : c + step]

    stack(own, own_split)
    both[0:vectors] = own[...]
    both[vectors:] = prev[...]
    offset[...] = energies[...] * own[...] - exact(beta_prev[...], prev[...], NN)
    early[p] = exact(own[...], both[...], NT)

    pl.semaphore_wait(barrier, greeted)

    far_copy = send(basis_hbm, far, far_sem.at[0], far_sem.at[1], at(g, p - g))

    @pl.when(g != 0)
    def _():
        far_copy.start()

    @pl.when(g == 0)
    def _():
        far[...] = own[...]

    early_copies = [
        send(early.at[p], early.at[p], early_send.at[d], early_recv.at[d], at(g, p + d))
        for d in range(1, segs)
    ]
    for copy in early_copies:
        copy.start()

    def backward(k, carry):
        tile_copy(k).wait()
        products[k] = multiply(own_split[rows[0, k]], k, NN)
        return carry

    lax.fori_loop(0, slots, backward, 0)
    scatter(cols, back)

    back_copies = []
    for d in range(groups):
        h = lax.rem(g + d, groups)
        back_copies.append(
            send(back.at[h], arrived.at[d], back_send.at[d], back_recv.at[d], at(h, p + g))
        )
    for copy in back_copies[1:]:
        copy.start()

    @pl.when(g != 0)
    def _():
        back_copies[0].start()

    @pl.when(g == 0)
    def _():
        arrived[0] = back[g]

    @pl.when(g != 0)
    def _():
        far_copy.wait()

    stack(far, far_split)

    def forward(k, carry):
        products[k] = multiply(far_split[cols[0, k]], k, NT)
        return carry

    lax.fori_loop(0, slots, forward, 0)
    scatter(rows, forth)

    forth_copies = []
    for d in range(1, groups):
        h = lax.rem(g + d, groups)
        forth_copies.append(
            send(forth.at[h], arrived.at[groups + d - 1], forth_send.at[d], forth_recv.at[d], at(h, p))
        )
    for copy in forth_copies:
        copy.start()
    for copy in forth_copies + back_copies[1:]:
        copy.wait()

    @pl.when(g != 0)
    def _():
        back_copies[0].wait()

    mine = forth[g]
    for d in range(2 * groups - 1):
        mine = mine + arrived[d]
    gathered[g] = mine

    gather_copies = [
        send(gathered.at[g], gathered.at[g], gather_send.at[d], gather_recv.at[d], at(g + d, p))
        for d in range(1, groups)
    ]
    for copy in gather_copies:
        copy.start()
    for copy in gather_copies:
        copy.wait()

    for h in range(groups):
        lanes = slice(h * part, (h + 1) * part)
        both[vectors:, lanes] = gathered[h] + offset[:, lanes]
    late[p] = exact(both[vectors:], both[...], NT)

    late_copies = [
        send(late.at[p], late.at[p], late_send.at[d], late_recv.at[d], at(g, p + d))
        for d in range(1, segs)
    ]
    for copy in late_copies:
        copy.start()
    for copy in early_copies:
        copy.wait()
    before = early[0]
    for s in range(1, segs):
        before = before + early[s]
    basis_basis, basis_prev = before[:, :vectors], before[:, vectors:]
    shift = exact(beta_prev[...], basis_prev, NT)
    for copy in late_copies:
        copy.wait()
    after = late[0]
    for s in range(1, segs):
        after = after + late[s]
    rest_basis, rest_rest = after[:, :vectors], after[:, vectors:]

    alpha_t = (rest_basis + shift) / total
    alpha_ref[...] = alpha_t.T
    gram = (
        rest_rest
        + exact(exact(alpha_t, basis_basis, NN) - rest_basis, alpha_t, NT)
        - exact(alpha_t, rest_basis, NT)
    ) / total
    residual = both[vectors:] - exact(alpha_t, own[...], NN)
    upper, inverse = factored(gram)
    beta_ref[...] = upper.T
    next_ref[...] = exact(inverse, residual, NN)


def shards(groups, segs, tiles, tile_row, tile_col, tile_count, energies, basis, prev_basis, beta_prev):
    slots, width = tiles.shape[2], tiles.shape[-1]
    vectors, length = basis.shape
    sides, part = length // width, length // groups
    dma = pltpu.SemaphoreType.DMA
    block = (vectors, length)
    return pl.pallas_call(
        functools.partial(kernel, groups, segs),
        out_shape=(
            jax.ShapeDtypeStruct(block, f32),
            jax.ShapeDtypeStruct((vectors, vectors), f32),
            jax.ShapeDtypeStruct((vectors, vectors), f32),
        ),
        in_specs=[pl.BlockSpec(memory_space=pl.ANY)] * 8,
        out_specs=tuple(pl.BlockSpec(memory_space=pltpu.VMEM) for _ in range(3)),
        scratch_shapes=[
            pltpu.VMEM((slots, width, width), f32),
            pltpu.SMEM((1, slots), jnp.int32),
            pltpu.SMEM((1, slots), jnp.int32),
            pltpu.SMEM((1, 1), jnp.int32),
            pltpu.VMEM((1, length), f32),
            pltpu.VMEM(block, f32),
            pltpu.VMEM(block, f32),
            pltpu.VMEM(block, f32),
            pltpu.VMEM((vectors, vectors), f32),
            pltpu.VMEM((sides, 2 * vectors, width), bf16),
            pltpu.VMEM((sides, 2 * vectors, width), bf16),
            pltpu.VMEM((slots, vectors, width), f32),
            pltpu.VMEM((groups, vectors, part), f32),
            pltpu.VMEM((groups, vectors, part), f32),
            pltpu.VMEM((2 * groups - 1, vectors, part), f32),
            pltpu.VMEM((groups, vectors, part), f32),
            pltpu.VMEM(block, f32),
            pltpu.VMEM((2 * vectors, length), f32),
            pltpu.VMEM((segs, vectors, 2 * vectors), f32),
            pltpu.VMEM((segs, vectors, 2 * vectors), f32),
            dma((7,)), dma((slots,)), dma((2,)),
            dma((groups,)), dma((groups,)), dma((groups,)), dma((groups,)),
            dma((groups,)), dma((groups,)),
            dma((segs,)), dma((segs,)), dma((segs,)), dma((segs,)),
        ],
        compiler_params=pltpu.CompilerParams(collective_id=0, has_side_effects=True),
    )(
        tiles.reshape(slots, width, width),
        tile_row.reshape(1, slots),
        tile_col.reshape(1, slots),
        tile_count.reshape(1, 1),
        energies.reshape(1, length),
        basis,
        prev_basis,
        beta_prev,
    )


def solution(mesh):
    groups, segs = mesh.shape["grp"], mesh.shape["pos"]
    in_specs = (
        P("grp", "pos", None, None, None),
        P("grp", "pos", None),
        P("grp", "pos", None),
        P("grp", "pos"),
        P("pos"),
        P(None, "pos"),
        P(None, "pos"),
        P(),
    )
    out_specs = (P(None, "pos"), P(), P())
    return jax.shard_map(
        functools.partial(shards, groups, segs),
        mesh=mesh, in_specs=in_specs, out_specs=out_specs, check_vma=False,
    )
```

```python
import functools

import jax
import jax.numpy as jnp
from jax import lax
from jax.experimental import pallas as pl
from jax.experimental.pallas import tpu as pltpu
from jax.sharding import PartitionSpec as P

MESH = pl.DeviceIdType.MESH
NT = (((1,), (1,)), ((), ()))
NN = (((1,), (0,)), ((), ()))
f32 = jnp.float32
bf16 = jnp.bfloat16


def exact(left, right, dims):
    return lax.dot_general(
        left, right, dims, precision=lax.Precision.HIGHEST, preferred_element_type=f32
    )


def split(values):
    high = values.astype(bf16)
    return high, (values - high.astype(f32)).astype(bf16)


def factored(gram):
    n = gram.shape[0]
    wide = jnp.concatenate([gram, jnp.eye(n, dtype=f32)], axis=1)
    row_at = lax.broadcasted_iota(jnp.int32, (n, 1), 0)
    done = jnp.zeros((n, 2 * n), f32)
    for j in range(n):
        column = wide[:, j : j + 1]
        scale = lax.rsqrt(wide[j : j + 1, j : j + 1])
        pivot = wide[j : j + 1, :] * scale
        done = jnp.where(row_at == j, pivot, done)
        wide = wide - jnp.where(row_at > j, column * scale, 0.0) * pivot
    return done[:, :n], done[:, n:]


def kernel(
    groups, segs,
    tiles_hbm, row_hbm, col_hbm, count_hbm, energies_hbm, basis_hbm, prev_hbm, beta_prev_hbm,
    rest_ref, sums_ref,
    tiles, rows, cols, count, energies, own, far, prev, beta_prev,
    own_split, far_split, products, back, forth, arrived, gathered, offset, both, early, late,
    in_sem, tile_sem, far_sem, back_send, back_recv, forth_send, forth_recv,
    gather_send, gather_recv, early_send, early_recv, late_send, late_recv,
):
    g, p = lax.axis_index("grp"), lax.axis_index("pos")
    slots, width = tiles.shape[0], tiles.shape[-1]
    vectors, length = own.shape
    sides = length // width
    part = length // groups

    def at(group, pos):
        return (lax.rem(group + groups, groups), lax.rem(pos + segs, segs))

    def send(src, dst, send_sem, recv_sem, to):
        return pltpu.make_async_remote_copy(
            src_ref=src, dst_ref=dst, send_sem=send_sem, recv_sem=recv_sem,
            device_id=to, device_id_type=MESH,
        )

    small = [
        pltpu.make_async_copy(src, dst, in_sem.at[i])
        for i, (src, dst) in enumerate([
            (basis_hbm, own), (prev_hbm, prev), (energies_hbm, energies),
            (beta_prev_hbm, beta_prev), (row_hbm, rows), (col_hbm, cols), (count_hbm, count),
        ])
    ]
    for copy in small:
        copy.start()

    def tile_copy(k):
        return pltpu.make_async_copy(tiles_hbm.at[k], tiles.at[k], tile_sem.at[k])

    for k in range(slots):
        tile_copy(k).start()

    barrier = pltpu.get_barrier_semaphore()
    greeted = 0
    for d in range(1, segs):
        pl.semaphore_signal(barrier, inc=1, device_id=at(g, p + d), device_id_type=MESH)
        greeted += 1
    for d in range(1, groups):
        pl.semaphore_signal(barrier, inc=1, device_id=at(g + d, p), device_id_type=MESH)
        source = lax.rem(g - d + groups, groups)
        pl.semaphore_signal(barrier, inc=1, device_id=at(source, p - source), device_id_type=MESH)
        greeted += 2

    for copy in small:
        copy.wait()

    def stack(ref, out):
        for t in range(sides):
            high, low = split(ref[:, t * width : (t + 1) * width])
            out[t] = jnp.concatenate([high, low], axis=0)

    def multiply(picked, k, dims):
        high, low = split(tiles[k])
        both_parts = lax.dot_general(picked, high, dims, preferred_element_type=f32)
        both_parts += lax.dot_general(picked, low, dims, preferred_element_type=f32)
        return both_parts[:vectors] + both_parts[vectors:]

    def scatter(index, out):
        for t in range(sides):
            value = jnp.zeros((vectors, width), f32)
            for k in range(slots):
                live = jnp.logical_and(index[0, k] == t, k < count[0, 0])
                value = value + products[k] * jnp.where(live, 1.0, 0.0).astype(f32)
            step = min(width, part)
            for c in range(0, width, step):
                lane = t * width + c
                out[lane // part, :, lane % part : lane % part + step] = value[:, c : c + step]

    stack(own, own_split)
    both[0:vectors] = own[...]
    both[vectors:] = prev[...]
    offset[...] = energies[...] * own[...] - exact(beta_prev[...], prev[...], NN)
    early[p] = exact(own[...], both[...], NT)

    pl.semaphore_wait(barrier, greeted)

    far_copy = send(basis_hbm, far, far_sem.at[0], far_sem.at[1], at(g, p - g))

    @pl.when(g != 0)
    def _():
        far_copy.start()

    @pl.when(g == 0)
    def _():
        far[...] = own[...]

    early_copies = [
        send(early.at[p], early.at[p], early_send.at[d], early_recv.at[d], at(g, p + d))
        for d in range(1, segs)
    ]
    for copy in early_copies:
        copy.start()

    def backward(k, carry):
        tile_copy(k).wait()
        products[k] = multiply(own_split[rows[0, k]], k, NN)
        return carry

    lax.fori_loop(0, slots, backward, 0)
    scatter(cols, back)

    back_copies = []
    for d in range(groups):
        h = lax.rem(g + d, groups)
        back_copies.append(
            send(back.at[h], arrived.at[d], back_send.at[d], back_recv.at[d], at(h, p + g))
        )
    for copy in back_copies[1:]:
        copy.start()

    @pl.when(g != 0)
    def _():
        back_copies[0].start()

    @pl.when(g == 0)
    def _():
        arrived[0] = back[g]

    @pl.when(g != 0)
    def _():
        far_copy.wait()

    stack(far, far_split)

    def forward(k, carry):
        products[k] = multiply(far_split[cols[0, k]], k, NT)
        return carry

    lax.fori_loop(0, slots, forward, 0)
    scatter(rows, forth)

    forth_copies = []
    for d in range(1, groups):
        h = lax.rem(g + d, groups)
        forth_copies.append(
            send(forth.at[h], arrived.at[groups + d - 1], forth_send.at[d], forth_recv.at[d], at(h, p))
        )
    for copy in forth_copies:
        copy.start()
    for copy in forth_copies + back_copies[1:]:
        copy.wait()

    @pl.when(g != 0)
    def _():
        back_copies[0].wait()

    mine = forth[g]
    for d in range(2 * groups - 1):
        mine = mine + arrived[d]
    gathered[g] = mine

    gather_copies = [
        send(gathered.at[g], gathered.at[g], gather_send.at[d], gather_recv.at[d], at(g + d, p))
        for d in range(1, groups)
    ]
    for copy in gather_copies:
        copy.start()
    for copy in gather_copies:
        copy.wait()

    for h in range(groups):
        lanes = slice(h * part, (h + 1) * part)
        both[vectors:, lanes] = gathered[h] + offset[:, lanes]
    late[p] = exact(both[vectors:], both[...], NT)

    late_copies = [
        send(late.at[p], late.at[p], late_send.at[d], late_recv.at[d], at(g, p + d))
        for d in range(1, segs)
    ]
    for copy in late_copies:
        copy.start()
    for copy in early_copies:
        copy.wait()
    before = early[0]
    for s in range(1, segs):
        before = before + early[s]
    for copy in late_copies:
        copy.wait()
    after = late[0]
    for s in range(1, segs):
        after = after + late[s]
    sums_ref[0] = before
    sums_ref[1] = after
    rest_ref[...] = both[vectors:]


def finish(total, rest_ref, basis_ref, sums_ref, beta_prev_ref, next_ref, alpha_ref, beta_ref):
    vectors = basis_ref.shape[0]
    basis_basis, basis_prev = sums_ref[0, :, :vectors], sums_ref[0, :, vectors:]
    rest_basis, rest_rest = sums_ref[1, :, :vectors], sums_ref[1, :, vectors:]
    alpha_t = (rest_basis + exact(beta_prev_ref[...], basis_prev, NT)) / total
    alpha_ref[...] = alpha_t.T
    gram = (
        rest_rest
        + exact(exact(alpha_t, basis_basis, NN) - rest_basis, alpha_t, NT)
        - exact(alpha_t, rest_basis, NT)
    ) / total
    residual = rest_ref[...] - exact(alpha_t, basis_ref[...], NN)
    upper, inverse = factored(gram)
    beta_ref[...] = upper.T
    next_ref[...] = exact(inverse, residual, NN)


def shards(groups, segs, tiles, tile_row, tile_col, tile_count, energies, basis, prev_basis, beta_prev):
    slots, width = tiles.shape[2], tiles.shape[-1]
    vectors, length = basis.shape
    sides, part = length // width, length // groups
    dma = pltpu.SemaphoreType.DMA
    block = (vectors, length)
    vmem = pl.BlockSpec(memory_space=pltpu.VMEM)
    rest, sums = pl.pallas_call(
        functools.partial(kernel, groups, segs),
        out_shape=(
            jax.ShapeDtypeStruct(block, f32),
            jax.ShapeDtypeStruct((2, vectors, 2 * vectors), f32),
        ),
        in_specs=[pl.BlockSpec(memory_space=pltpu.HBM)] * 8,
        out_specs=(vmem, vmem),
        scratch_shapes=[
            pltpu.VMEM((slots, width, width), f32),
            pltpu.SMEM((1, slots), jnp.int32),
            pltpu.SMEM((1, slots), jnp.int32),
            pltpu.SMEM((1, 1), jnp.int32),
            pltpu.VMEM((1, length), f32),
            pltpu.VMEM(block, f32),
            pltpu.VMEM(block, f32),
            pltpu.VMEM(block, f32),
            pltpu.VMEM((vectors, vectors), f32),
            pltpu.VMEM((sides, 2 * vectors, width), bf16),
            pltpu.VMEM((sides, 2 * vectors, width), bf16),
            pltpu.VMEM((slots, vectors, width), f32),
            pltpu.VMEM((groups, vectors, part), f32),
            pltpu.VMEM((groups, vectors, part), f32),
            pltpu.VMEM((2 * groups - 1, vectors, part), f32),
            pltpu.VMEM((groups, vectors, part), f32),
            pltpu.VMEM(block, f32),
            pltpu.VMEM((2 * vectors, length), f32),
            pltpu.VMEM((segs, vectors, 2 * vectors), f32),
            pltpu.VMEM((segs, vectors, 2 * vectors), f32),
            dma((7,)), dma((slots,)), dma((2,)),
            dma((groups,)), dma((groups,)), dma((groups,)), dma((groups,)),
            dma((groups,)), dma((groups,)),
            dma((segs,)), dma((segs,)), dma((segs,)), dma((segs,)),
        ],
        compiler_params=pltpu.CompilerParams(collective_id=0, has_side_effects=True),
    )(
        tiles.reshape(slots, width, width),
        tile_row.reshape(1, slots),
        tile_col.reshape(1, slots),
        tile_count.reshape(1, 1),
        energies.reshape(1, length),
        basis,
        prev_basis,
        beta_prev,
    )
    return pl.pallas_call(
        functools.partial(finish, float(length * segs)),
        out_shape=(
            jax.ShapeDtypeStruct(block, f32),
            jax.ShapeDtypeStruct((vectors, vectors), f32),
            jax.ShapeDtypeStruct((vectors, vectors), f32),
        ),
        in_specs=[vmem] * 4,
        out_specs=(vmem, vmem, vmem),
    )(rest, basis, sums, beta_prev)


def solution(mesh):
    groups, segs = mesh.shape["grp"], mesh.shape["pos"]
    in_specs = (
        P("grp", "pos", None, None, None),
        P("grp", "pos", None),
        P("grp", "pos", None),
        P("grp", "pos"),
        P("pos"),
        P(None, "pos"),
        P(None, "pos"),
        P(),
    )
    out_specs = (P(None, "pos"), P(), P())
    return jax.shard_map(
        functools.partial(shards, groups, segs),
        mesh=mesh, in_specs=in_specs, out_specs=out_specs, check_vma=False,
    )
```

```python
import functools

import jax
import jax.numpy as jnp
from jax import lax
from jax.experimental import pallas as pl
from jax.experimental.pallas import tpu as pltpu
from jax.sharding import PartitionSpec as P

MESH = pl.DeviceIdType.MESH
NT = (((1,), (1,)), ((), ()))
NN = (((1,), (0,)), ((), ()))
f32 = jnp.float32
bf16 = jnp.bfloat16


def exact(left, right, dims):
    return lax.dot_general(
        left, right, dims, precision=lax.Precision.HIGHEST, preferred_element_type=f32
    )


def split(values):
    high = values.astype(bf16)
    return high, (values - high.astype(f32)).astype(bf16)


def packed(values):
    half = values.shape[0] // 2
    return jnp.concatenate([values[:half], values[half:]], axis=1)


def unpacked(values):
    half = values.shape[1] // 2
    return jnp.concatenate([values[:, :half], values[:, half:]], axis=0)


def factored(gram):
    n = gram.shape[0]
    wide = jnp.concatenate([gram, jnp.eye(n, dtype=f32)], axis=1)
    row_at = lax.broadcasted_iota(jnp.int32, (n, 1), 0)
    columns = [jnp.broadcast_to(gram[:, k : k + 1], (n, 2 * n)) for k in range(n)]
    done = jnp.zeros((n, 2 * n), f32)
    for j in range(n):
        corner = columns[j][j : j + 1]
        inverse = 1.0 / corner
        row = wide[j : j + 1]
        done = jnp.where(row_at == j, row * lax.rsqrt(corner), done)
        for k in range(j + 1, n):
            columns[k] = columns[k] - columns[j] * (columns[k][j : j + 1] * inverse)
        wide = wide - columns[j] * (row * inverse)
    return done[:, :n], done[:, n:]


def kernel(
    groups, segs,
    tiles_hbm, row_hbm, col_hbm, count_hbm, energies_hbm, basis_hbm, prev_hbm, beta_prev_hbm,
    rest_hbm, sums_ref,
    tiles, rows, cols, count, energies, own, far, prev, beta_prev,
    own_split, far_split, products, back, forth, arrived, gathered, offset, both, early, late,
    in_sem, tile_sem, far_send, far_recv, back_send, back_recv, forth_send, forth_recv,
    gather_send, gather_recv, early_send, early_recv, late_send, late_recv,
):
    g, p = lax.axis_index("grp"), lax.axis_index("pos")
    slots, width = tiles.shape[0], tiles.shape[-1]
    vectors, length = own.shape
    sides = length // width
    part = length // groups

    def at(group, pos):
        return (lax.rem(group + groups, groups), lax.rem(pos + segs, segs))

    def send(src, dst, send_sem, recv_sem, to):
        return pltpu.make_async_remote_copy(
            src_ref=src, dst_ref=dst, send_sem=send_sem, recv_sem=recv_sem,
            device_id=to, device_id_type=MESH,
        )

    barrier = pltpu.get_barrier_semaphore()
    greeted = 0
    for d in range(1, segs):
        pl.semaphore_signal(barrier, inc=1, device_id=at(g, p + d), device_id_type=MESH)
        greeted += 1
    for d in range(1, groups):
        pl.semaphore_signal(barrier, inc=1, device_id=at(g + d, p), device_id_type=MESH)
        source = lax.rem(g - d + groups, groups)
        pl.semaphore_signal(barrier, inc=1, device_id=at(source, p - source), device_id_type=MESH)
        pl.semaphore_signal(barrier, inc=1, device_id=at(g + d, p + g), device_id_type=MESH)
        greeted += 3

    small = [
        pltpu.make_async_copy(src, dst, in_sem.at[i])
        for i, (src, dst) in enumerate([
            (basis_hbm, own), (prev_hbm, prev), (energies_hbm, energies),
            (beta_prev_hbm, beta_prev), (row_hbm, rows), (col_hbm, cols), (count_hbm, count),
        ])
    ]
    for copy in small:
        copy.start()

    def tile_copy(k):
        return pltpu.make_async_copy(tiles_hbm.at[k], tiles.at[k], tile_sem.at[k])

    for k in range(slots):
        tile_copy(k).start()

    def stack(ref, out):
        for t in range(sides):
            high, low = split(ref[:, t * width : (t + 1) * width])
            out[t] = jnp.concatenate([high, low], axis=0)

    def multiply(picked, k, dims):
        high, low = split(tiles[k])
        both_parts = lax.dot_general(picked, high, dims, preferred_element_type=f32)
        both_parts += lax.dot_general(picked, low, dims, preferred_element_type=f32)
        return both_parts[:vectors] + both_parts[vectors:]

    def scatter(index, out):
        for t in range(sides):
            value = jnp.zeros((vectors, width), f32)
            for k in range(slots):
                live = jnp.logical_and(index[0, k] == t, k < count[0, 0])
                value = value + products[k] * jnp.where(live, 1.0, 0.0).astype(f32)
            step = min(width, part)
            for c in range(0, width, step):
                lane = t * width + c
                out[lane // part, :, lane % part : lane % part + step] = value[:, c : c + step]

    pl.semaphore_wait(barrier, greeted)

    lanes = pl.ds(pl.multiple_of(g * part, part), part)
    far_copies = []
    for d in range(groups):
        other = lax.rem(g + d, groups)
        far_copies.append(
            send(
                basis_hbm.at[:, lanes], far.at[:, lanes], far_send.at[d], far_recv.at[d],
                at(other, p - other),
            )
        )
        pl.when(other != 0)(far_copies[d].start)

    for copy in small:
        copy.wait()

    @pl.when(g == 0)
    def _():
        far[...] = own[...]

    stack(own, own_split)
    both[0:vectors] = own[...]
    both[vectors:] = prev[...]
    early[p] = packed(exact(own[...], both[...], NT))

    early_copies = [
        send(early.at[p], early.at[p], early_send.at[d], early_recv.at[d], at(g, p + d))
        for d in range(1, segs)
    ]
    for copy in early_copies:
        copy.start()

    def backward(k, carry):
        tile_copy(k).wait()
        products[k] = multiply(own_split[rows[0, k]], k, NN)
        return carry

    lax.fori_loop(0, slots, backward, 0)
    scatter(cols, back)

    back_copies = []
    for d in range(groups):
        h = lax.rem(g + d, groups)
        back_copies.append(
            send(back.at[h], arrived.at[d], back_send.at[d], back_recv.at[d], at(h, p + g))
        )
    for copy in back_copies[1:]:
        copy.start()

    @pl.when(g != 0)
    def _():
        back_copies[0].start()

    @pl.when(g == 0)
    def _():
        arrived[0] = back[g]

    offset[...] = energies[...] * own[...] - exact(beta_prev[...], prev[...], NN)

    @pl.when(g != 0)
    def _():
        for copy in far_copies:
            copy.wait_recv()

    stack(far, far_split)

    def forward(k, carry):
        products[k] = multiply(far_split[cols[0, k]], k, NT)
        return carry

    lax.fori_loop(0, slots, forward, 0)
    scatter(rows, forth)

    forth_copies = []
    for d in range(1, groups):
        h = lax.rem(g + d, groups)
        forth_copies.append(
            send(forth.at[h], arrived.at[groups + d - 1], forth_send.at[d], forth_recv.at[d], at(h, p))
        )
    for copy in forth_copies:
        copy.start()
    for copy in forth_copies + back_copies[1:]:
        copy.wait_recv()

    pl.when(g != 0)(back_copies[0].wait_recv)

    mine = forth[g]
    for d in range(2 * groups - 1):
        mine = mine + arrived[d]
    gathered[g] = mine

    gather_copies = [
        send(gathered.at[g], gathered.at[g], gather_send.at[d], gather_recv.at[d], at(g + d, p))
        for d in range(1, groups)
    ]
    for copy in gather_copies:
        copy.start()
    for copy in gather_copies:
        copy.wait_recv()

    for h in range(groups):
        lanes = slice(h * part, (h + 1) * part)
        both[vectors:, lanes] = gathered[h] + offset[:, lanes]
    late[p] = packed(exact(both[vectors:], both[...], NT))

    late_copies = [
        send(late.at[p], late.at[p], late_send.at[d], late_recv.at[d], at(g, p + d))
        for d in range(1, segs)
    ]
    for copy in late_copies:
        copy.start()
    rest_copy = pltpu.make_async_copy(both.at[vectors:], rest_hbm, in_sem.at[0])
    rest_copy.start()
    for copy in early_copies:
        copy.wait_recv()
    before = early[0]
    for s in range(1, segs):
        before = before + early[s]
    for copy in early_copies + forth_copies + back_copies[1:] + gather_copies + late_copies:
        copy.wait_send()
    pl.when(g != 0)(back_copies[0].wait_send)
    for d in range(groups):
        pl.when(lax.rem(g + d, groups) != 0)(far_copies[d].wait_send)
    for copy in late_copies:
        copy.wait_recv()
    after = late[0]
    for s in range(1, segs):
        after = after + late[s]
    sums_ref[0] = before
    sums_ref[1] = after
    rest_copy.wait()


def finish(
    total, rest_hbm, basis_hbm, sums_ref, beta_prev_ref, next_ref, alpha_ref, beta_ref, rest, basis, sem
):
    copies = [
        pltpu.make_async_copy(rest_hbm, rest, sem.at[0]),
        pltpu.make_async_copy(basis_hbm, basis, sem.at[1]),
    ]
    for copy in copies:
        copy.start()
    vectors = beta_prev_ref.shape[0]
    before, after = unpacked(sums_ref[0]), unpacked(sums_ref[1])
    basis_basis, basis_prev = before[:, :vectors], before[:, vectors:]
    rest_basis, rest_rest = after[:, :vectors], after[:, vectors:]
    alpha_t = (rest_basis + exact(beta_prev_ref[...], basis_prev, NT)) / total
    alpha_ref[...] = alpha_t.T
    gram = (
        rest_rest
        + exact(exact(alpha_t, basis_basis, NN) - rest_basis, alpha_t, NT)
        - exact(alpha_t, rest_basis, NT)
    ) / total
    upper, inverse = factored(gram)
    beta_ref[...] = upper.T
    for copy in copies:
        copy.wait()
    residual = rest[...] - exact(alpha_t, basis[...], NN)
    next_ref[...] = exact(inverse, residual, NN)


def shards(groups, segs, tiles, tile_row, tile_col, tile_count, energies, basis, prev_basis, beta_prev):
    slots, width = tiles.shape[2], tiles.shape[-1]
    vectors, length = basis.shape
    sides, part = length // width, length // groups
    dma = pltpu.SemaphoreType.DMA
    block = (vectors, length)
    vmem = pl.BlockSpec(memory_space=pltpu.VMEM)
    rest, sums = pl.pallas_call(
        functools.partial(kernel, groups, segs),
        out_shape=(
            jax.ShapeDtypeStruct(block, f32),
            jax.ShapeDtypeStruct((2, vectors // 2, 4 * vectors), f32),
        ),
        in_specs=[pl.BlockSpec(memory_space=pltpu.HBM)] * 8,
        out_specs=(pl.BlockSpec(memory_space=pltpu.HBM), vmem),
        scratch_shapes=[
            pltpu.VMEM((slots, width, width), f32),
            pltpu.SMEM((1, slots), jnp.int32),
            pltpu.SMEM((1, slots), jnp.int32),
            pltpu.SMEM((1, 1), jnp.int32),
            pltpu.VMEM((1, length), f32),
            pltpu.VMEM(block, f32),
            pltpu.VMEM(block, f32),
            pltpu.VMEM(block, f32),
            pltpu.VMEM((vectors, vectors), f32),
            pltpu.VMEM((sides, 2 * vectors, width), bf16),
            pltpu.VMEM((sides, 2 * vectors, width), bf16),
            pltpu.VMEM((slots, vectors, width), f32),
            pltpu.VMEM((groups, vectors, part), f32),
            pltpu.VMEM((groups, vectors, part), f32),
            pltpu.VMEM((2 * groups - 1, vectors, part), f32),
            pltpu.VMEM((groups, vectors, part), f32),
            pltpu.VMEM(block, f32),
            pltpu.VMEM((2 * vectors, length), f32),
            pltpu.VMEM((segs, vectors // 2, 4 * vectors), f32),
            pltpu.VMEM((segs, vectors // 2, 4 * vectors), f32),
            dma((7,)), dma((slots,)), dma((groups,)), dma((groups,)),
            dma((groups,)), dma((groups,)), dma((groups,)), dma((groups,)),
            dma((groups,)), dma((groups,)),
            dma((segs,)), dma((segs,)), dma((segs,)), dma((segs,)),
        ],
        compiler_params=pltpu.CompilerParams(collective_id=0, has_side_effects=True),
    )(
        tiles.reshape(slots, width, width),
        tile_row.reshape(1, slots),
        tile_col.reshape(1, slots),
        tile_count.reshape(1, 1),
        energies.reshape(1, length),
        basis,
        prev_basis,
        beta_prev,
    )
    return pl.pallas_call(
        functools.partial(finish, float(length * segs)),
        out_shape=(
            jax.ShapeDtypeStruct(block, f32),
            jax.ShapeDtypeStruct((vectors, vectors), f32),
            jax.ShapeDtypeStruct((vectors, vectors), f32),
        ),
        in_specs=[pl.BlockSpec(memory_space=pltpu.HBM)] * 2 + [vmem] * 2,
        out_specs=(vmem, vmem, vmem),
        scratch_shapes=[pltpu.VMEM(block, f32), pltpu.VMEM(block, f32), dma((2,))],
    )(rest, basis, sums, beta_prev)


def solution(mesh):
    groups, segs = mesh.shape["grp"], mesh.shape["pos"]
    in_specs = (
        P("grp", "pos", None, None, None),
        P("grp", "pos", None),
        P("grp", "pos", None),
        P("grp", "pos"),
        P("pos"),
        P(None, "pos"),
        P(None, "pos"),
        P(),
    )
    out_specs = (P(None, "pos"), P(), P())
    return jax.shard_map(
        functools.partial(shards, groups, segs),
        mesh=mesh, in_specs=in_specs, out_specs=out_specs, check_vma=False,
    )
```

```python
import functools

import jax
import jax.numpy as jnp
from jax import lax
from jax.experimental import pallas as pl
from jax.experimental.pallas import tpu as pltpu
from jax.sharding import PartitionSpec as P

MESH = pl.DeviceIdType.MESH
NT = (((1,), (1,)), ((), ()))
NN = (((1,), (0,)), ((), ()))
f32 = jnp.float32
bf16 = jnp.bfloat16


def exact(left, right, dims):
    return lax.dot_general(
        left, right, dims, precision=lax.Precision.HIGHEST, preferred_element_type=f32
    )


def split(values):
    high = values.astype(bf16)
    return high, (values - high.astype(f32)).astype(bf16)


def packed(values):
    half = values.shape[0] // 2
    return jnp.concatenate([values[:half], values[half:]], axis=1)


def unpacked(values):
    half = values.shape[1] // 2
    return jnp.concatenate([values[:, :half], values[:, half:]], axis=0)


def factored(gram):
    n = gram.shape[0]
    wide = jnp.concatenate([gram, jnp.eye(n, dtype=f32)], axis=1)
    row_at = lax.broadcasted_iota(jnp.int32, (n, 1), 0)
    columns = [jnp.broadcast_to(gram[:, k : k + 1], (n, 2 * n)) for k in range(n)]
    done = jnp.zeros((n, 2 * n), f32)
    for j in range(n):
        corner = columns[j][j : j + 1]
        inverse = 1.0 / corner
        row = wide[j : j + 1]
        done = jnp.where(row_at == j, row * lax.rsqrt(corner), done)
        for k in range(j + 1, n):
            columns[k] = columns[k] - columns[j] * (columns[k][j : j + 1] * inverse)
        wide = wide - columns[j] * (row * inverse)
    return done[:, :n], done[:, n:]


def kernel(
    groups, segs,
    tiles_hbm, row_hbm, col_hbm, count_hbm, energies_hbm, basis_hbm, prev_hbm, beta_prev_hbm,
    rest_hbm, sums_ref,
    tiles, rows, cols, count, energies, own, far, prev, beta_prev,
    own_split, far_split, products, back, forth, arrived, gathered, offset, both, pair, late,
    in_sem, tile_sem, far_send, far_recv, back_send, back_recv, forth_send, forth_recv,
    gather_send, gather_recv, pair_sem, late_send, late_recv,
):
    g, p = lax.axis_index("grp"), lax.axis_index("pos")
    slots, width = tiles.shape[0], tiles.shape[-1]
    vectors, length = own.shape
    sides = length // width
    part = length // groups

    def at(group, pos):
        return (lax.rem(group + groups, groups), lax.rem(pos + segs, segs))

    def send(src, dst, send_sem, recv_sem, to):
        return pltpu.make_async_remote_copy(
            src_ref=src, dst_ref=dst, send_sem=send_sem, recv_sem=recv_sem,
            device_id=to, device_id_type=MESH,
        )

    barrier = pltpu.get_barrier_semaphore()
    greeted = 0
    for d in range(1, segs):
        pl.semaphore_signal(barrier, inc=1, device_id=at(g, p + d), device_id_type=MESH)
        greeted += 1
    for d in range(1, groups):
        pl.semaphore_signal(barrier, inc=1, device_id=at(g + d, p), device_id_type=MESH)
        source = lax.rem(g - d + groups, groups)
        pl.semaphore_signal(barrier, inc=1, device_id=at(source, p - source), device_id_type=MESH)
        pl.semaphore_signal(barrier, inc=1, device_id=at(g + d, p + g), device_id_type=MESH)
        greeted += 3

    small = [
        pltpu.make_async_copy(src, dst, in_sem.at[i])
        for i, (src, dst) in enumerate([
            (basis_hbm, own), (prev_hbm, prev), (energies_hbm, energies),
            (beta_prev_hbm, beta_prev), (row_hbm, rows), (col_hbm, cols), (count_hbm, count),
        ])
    ]
    for copy in small:
        copy.start()

    def tile_copy(k):
        return pltpu.make_async_copy(tiles_hbm.at[k], tiles.at[k], tile_sem.at[k])

    for k in range(slots):
        tile_copy(k).start()

    def stack(ref, out):
        for t in range(sides):
            high, low = split(ref[:, t * width : (t + 1) * width])
            out[t] = jnp.concatenate([high, low], axis=0)

    def multiply(picked, k, dims):
        high, low = split(tiles[k])
        both_parts = lax.dot_general(picked, high, dims, preferred_element_type=f32)
        both_parts += lax.dot_general(picked, low, dims, preferred_element_type=f32)
        return both_parts[:vectors] + both_parts[vectors:]

    def scatter(index, out):
        for t in range(sides):
            value = jnp.zeros((vectors, width), f32)
            for k in range(slots):
                live = jnp.logical_and(index[0, k] == t, k < count[0, 0])
                value = value + products[k] * jnp.where(live, 1.0, 0.0).astype(f32)
            step = min(width, part)
            for c in range(0, width, step):
                lane = t * width + c
                out[lane // part, :, lane % part : lane % part + step] = value[:, c : c + step]

    for copy in small:
        copy.wait()

    @pl.when(g == 0)
    def _():
        far[...] = own[...]

    stack(own, own_split)
    def backward(k, carry):
        tile_copy(k).wait()
        products[k] = multiply(own_split[rows[0, k]], k, NN)
        return carry

    lax.fori_loop(0, slots, backward, 0)
    scatter(cols, back)

    pl.semaphore_wait(barrier, greeted)

    lanes = pl.ds(pl.multiple_of(g * part, part), part)
    far_copies = []
    for d in range(groups):
        other = lax.rem(g + d, groups)
        far_copies.append(
            send(
                basis_hbm.at[:, lanes], far.at[:, lanes], far_send.at[d], far_recv.at[d],
                at(other, p - other),
            )
        )
        pl.when(other != 0)(far_copies[d].start)

    back_copies = []
    for d in range(groups):
        h = lax.rem(g + d, groups)
        back_copies.append(
            send(back.at[h], arrived.at[d], back_send.at[d], back_recv.at[d], at(h, p + g))
        )
    for copy in back_copies[1:]:
        copy.start()

    @pl.when(g != 0)
    def _():
        back_copies[0].start()

    @pl.when(g == 0)
    def _():
        arrived[0] = back[g]

    both[0:vectors] = own[...]
    both[vectors:] = prev[...]
    pair_slot, chip = lax.rem(p, 2), p // 2
    pair[pair_slot, :, : 4 * vectors] = packed(exact(own[...], both[...], NT))
    offset[...] = energies[...] * own[...] - exact(beta_prev[...], prev[...], NN)

    @pl.when(g != 0)
    def _():
        for copy in far_copies:
            copy.wait_recv()

    stack(far, far_split)

    def forward(k, carry):
        products[k] = multiply(far_split[cols[0, k]], k, NT)
        return carry

    lax.fori_loop(0, slots, forward, 0)
    scatter(rows, forth)

    forth_copies = []
    for d in range(1, groups):
        h = lax.rem(g + d, groups)
        forth_copies.append(
            send(forth.at[h], arrived.at[groups + d - 1], forth_send.at[d], forth_recv.at[d], at(h, p))
        )
    for copy in forth_copies:
        copy.start()
    for copy in forth_copies + back_copies[1:]:
        copy.wait_recv()

    pl.when(g != 0)(back_copies[0].wait_recv)

    mine = forth[g]
    for d in range(2 * groups - 1):
        mine = mine + arrived[d]
    gathered[g] = mine

    gather_copies = [
        send(gathered.at[g], gathered.at[g], gather_send.at[d], gather_recv.at[d], at(g + d, p))
        for d in range(1, groups)
    ]
    for copy in gather_copies:
        copy.start()
    for copy in gather_copies:
        copy.wait_recv()

    for h in range(groups):
        lanes = slice(h * part, (h + 1) * part)
        both[vectors:, lanes] = gathered[h] + offset[:, lanes]
    pair[pair_slot, :, 4 * vectors :] = packed(exact(both[vectors:], both[...], NT))

    pair_copy = send(
        pair.at[pair_slot], pair.at[pair_slot], pair_sem.at[0], pair_sem.at[1],
        at(g, p + 1 - 2 * pair_slot),
    )
    pair_copy.start()
    rest_copy = pltpu.make_async_copy(both.at[vectors:], rest_hbm, in_sem.at[0])
    rest_copy.start()
    pair_copy.wait_recv()
    late[chip] = pair[0] + pair[1]
    late_copies = [
        send(late.at[chip], late.at[chip], late_send.at[d], late_recv.at[d], at(g, p + 2 * d))
        for d in range(1, segs // 2)
    ]
    for copy in late_copies:
        copy.start()
    for copy in forth_copies + back_copies[1:] + gather_copies + [pair_copy]:
        copy.wait_send()
    pl.when(g != 0)(back_copies[0].wait_send)
    for d in range(groups):
        pl.when(lax.rem(g + d, groups) != 0)(far_copies[d].wait_send)
    for copy in late_copies:
        copy.wait()
    after = late[0]
    for s in range(1, segs // 2):
        after = after + late[s]
    sums_ref[...] = after
    rest_copy.wait()


def finish(
    total, rest_hbm, basis_hbm, sums_ref, beta_prev_ref, next_ref, alpha_ref, beta_ref, rest, basis, sem
):
    copies = [
        pltpu.make_async_copy(rest_hbm, rest, sem.at[0]),
        pltpu.make_async_copy(basis_hbm, basis, sem.at[1]),
    ]
    for copy in copies:
        copy.start()
    vectors = beta_prev_ref.shape[0]
    before = unpacked(sums_ref[:, : 4 * vectors])
    after = unpacked(sums_ref[:, 4 * vectors :])
    basis_basis, basis_prev = before[:, :vectors], before[:, vectors:]
    rest_basis, rest_rest = after[:, :vectors], after[:, vectors:]
    alpha_t = (rest_basis + exact(beta_prev_ref[...], basis_prev, NT)) / total
    alpha_ref[...] = alpha_t.T
    gram = (
        rest_rest
        + exact(exact(alpha_t, basis_basis, NN) - rest_basis, alpha_t, NT)
        - exact(alpha_t, rest_basis, NT)
    ) / total
    upper, inverse = factored(gram)
    beta_ref[...] = upper.T
    for copy in copies:
        copy.wait()
    residual = rest[...] - exact(alpha_t, basis[...], NN)
    next_ref[...] = exact(inverse, residual, NN)


def shards(groups, segs, tiles, tile_row, tile_col, tile_count, energies, basis, prev_basis, beta_prev):
    slots, width = tiles.shape[2], tiles.shape[-1]
    vectors, length = basis.shape
    sides, part = length // width, length // groups
    dma = pltpu.SemaphoreType.DMA
    block = (vectors, length)
    vmem = pl.BlockSpec(memory_space=pltpu.VMEM)
    rest, sums = pl.pallas_call(
        functools.partial(kernel, groups, segs),
        out_shape=(
            jax.ShapeDtypeStruct(block, f32),
            jax.ShapeDtypeStruct((vectors // 2, 8 * vectors), f32),
        ),
        in_specs=[pl.BlockSpec(memory_space=pltpu.HBM)] * 8,
        out_specs=(pl.BlockSpec(memory_space=pltpu.HBM), vmem),
        scratch_shapes=[
            pltpu.VMEM((slots, width, width), f32),
            pltpu.SMEM((1, slots), jnp.int32),
            pltpu.SMEM((1, slots), jnp.int32),
            pltpu.SMEM((1, 1), jnp.int32),
            pltpu.VMEM((1, length), f32),
            pltpu.VMEM(block, f32),
            pltpu.VMEM(block, f32),
            pltpu.VMEM(block, f32),
            pltpu.VMEM((vectors, vectors), f32),
            pltpu.VMEM((sides, 2 * vectors, width), bf16),
            pltpu.VMEM((sides, 2 * vectors, width), bf16),
            pltpu.VMEM((slots, vectors, width), f32),
            pltpu.VMEM((groups, vectors, part), f32),
            pltpu.VMEM((groups, vectors, part), f32),
            pltpu.VMEM((2 * groups - 1, vectors, part), f32),
            pltpu.VMEM((groups, vectors, part), f32),
            pltpu.VMEM(block, f32),
            pltpu.VMEM((2 * vectors, length), f32),
            pltpu.VMEM((2, vectors // 2, 8 * vectors), f32),
            pltpu.VMEM((segs // 2, vectors // 2, 8 * vectors), f32),
            dma((7,)), dma((slots,)), dma((groups,)), dma((groups,)),
            dma((groups,)), dma((groups,)), dma((groups,)), dma((groups,)),
            dma((groups,)), dma((groups,)),
            dma((2,)), dma((segs // 2,)), dma((segs // 2,)),
        ],
        compiler_params=pltpu.CompilerParams(collective_id=0, has_side_effects=True),
    )(
        tiles.reshape(slots, width, width),
        tile_row.reshape(1, slots),
        tile_col.reshape(1, slots),
        tile_count.reshape(1, 1),
        energies.reshape(1, length),
        basis,
        prev_basis,
        beta_prev,
    )
    return pl.pallas_call(
        functools.partial(finish, float(length * segs)),
        out_shape=(
            jax.ShapeDtypeStruct(block, f32),
            jax.ShapeDtypeStruct((vectors, vectors), f32),
            jax.ShapeDtypeStruct((vectors, vectors), f32),
        ),
        in_specs=[pl.BlockSpec(memory_space=pltpu.HBM)] * 2 + [vmem] * 2,
        out_specs=(vmem, vmem, vmem),
        scratch_shapes=[pltpu.VMEM(block, f32), pltpu.VMEM(block, f32), dma((2,))],
    )(rest, basis, sums, beta_prev)


def solution(mesh):
    groups, segs = mesh.shape["grp"], mesh.shape["pos"]
    in_specs = (
        P("grp", "pos", None, None, None),
        P("grp", "pos", None),
        P("grp", "pos", None),
        P("grp", "pos"),
        P("pos"),
        P(None, "pos"),
        P(None, "pos"),
        P(),
    )
    out_specs = (P(None, "pos"), P(), P())
    return jax.shard_map(
        functools.partial(shards, groups, segs),
        mesh=mesh, in_specs=in_specs, out_specs=out_specs, check_vma=False,
    )
```

```python
import functools

import jax
import jax.numpy as jnp
from jax import lax
from jax.experimental import pallas as pl
from jax.experimental.pallas import tpu as pltpu
from jax.sharding import PartitionSpec as P

MESH = pl.DeviceIdType.MESH
NT = (((1,), (1,)), ((), ()))
NN = (((1,), (0,)), ((), ()))
f32 = jnp.float32
bf16 = jnp.bfloat16


def exact(left, right, dims):
    return lax.dot_general(
        left, right, dims, precision=lax.Precision.HIGHEST, preferred_element_type=f32
    )


def split(values):
    high = values.astype(bf16)
    return high, (values - high.astype(f32)).astype(bf16)


def packed(values):
    half = values.shape[0] // 2
    return jnp.concatenate([values[:half], values[half:]], axis=1)


def unpacked(values):
    half = values.shape[1] // 2
    return jnp.concatenate([values[:, :half], values[:, half:]], axis=0)


def factored(gram):
    n = gram.shape[0]
    wide = jnp.concatenate([gram, jnp.eye(n, dtype=f32)], axis=1)
    row_at = lax.broadcasted_iota(jnp.int32, (n, 1), 0)
    columns = [jnp.broadcast_to(gram[:, k : k + 1], (n, 2 * n)) for k in range(n)]
    done = jnp.zeros((n, 2 * n), f32)
    for j in range(n):
        corner = columns[j][j : j + 1]
        inverse = 1.0 / corner
        row = wide[j : j + 1]
        done = jnp.where(row_at == j, row * lax.rsqrt(corner), done)
        for k in range(j + 1, n):
            columns[k] = columns[k] - columns[j] * (columns[k][j : j + 1] * inverse)
        wide = wide - columns[j] * (row * inverse)
    return done[:, :n], done[:, n:]


def kernel(
    groups, segs,
    tiles_hbm, row_hbm, col_hbm, count_hbm, energies_hbm, basis_hbm, prev_hbm, beta_prev_hbm,
    rest_hbm, sums_ref,
    tiles, rows, cols, count, energies, own, far, prev, beta_prev,
    own_split, far_split, products, back, plane, forth, arrived, gathered, offset, both, pair, late,
    in_sem, tile_sem, far_send, far_recv, plane_send, plane_recv, back_send, back_recv, forth_send, forth_recv,
    gather_send, gather_recv, pair_sem, late_send, late_recv,
):
    g, p = lax.axis_index("grp"), lax.axis_index("pos")
    slots, width = tiles.shape[0], tiles.shape[-1]
    vectors, length = own.shape
    sides = length // width
    part = length // groups

    def at(group, pos):
        return (lax.rem(group + groups, groups), lax.rem(pos + segs, segs))

    def send(src, dst, send_sem, recv_sem, to):
        return pltpu.make_async_remote_copy(
            src_ref=src, dst_ref=dst, send_sem=send_sem, recv_sem=recv_sem,
            device_id=to, device_id_type=MESH,
        )

    barrier = pltpu.get_barrier_semaphore()
    greeted = 0
    for d in range(1, segs):
        pl.semaphore_signal(barrier, inc=1, device_id=at(g, p + d), device_id_type=MESH)
        greeted += 1
    for d in range(1, groups):
        pl.semaphore_signal(barrier, inc=1, device_id=at(g + d, p), device_id_type=MESH)
        pl.semaphore_signal(barrier, inc=1, device_id=at(g + d, p + g), device_id_type=MESH)
        greeted += 2

    small = [
        pltpu.make_async_copy(src, dst, in_sem.at[i])
        for i, (src, dst) in enumerate([
            (basis_hbm, own), (prev_hbm, prev), (energies_hbm, energies),
            (beta_prev_hbm, beta_prev), (row_hbm, rows), (col_hbm, cols), (count_hbm, count),
        ])
    ]
    for copy in small:
        copy.start()

    def tile_copy(k):
        return pltpu.make_async_copy(tiles_hbm.at[k], tiles.at[k], tile_sem.at[k])

    for k in range(slots):
        tile_copy(k).start()

    def stack(ref, out):
        for t in range(sides):
            high, low = split(ref[:, t * width : (t + 1) * width])
            out[t] = jnp.concatenate([high, low], axis=0)

    def multiply(picked, k, dims):
        high, low = split(tiles[k])
        both_parts = lax.dot_general(picked, high, dims, preferred_element_type=f32)
        both_parts += lax.dot_general(picked, low, dims, preferred_element_type=f32)
        return both_parts[:vectors] + both_parts[vectors:]

    def scatter(index, out):
        for t in range(sides):
            value = jnp.zeros((vectors, width), f32)
            for k in range(slots):
                live = jnp.logical_and(index[0, k] == t, k < count[0, 0])
                value = value + products[k] * jnp.where(live, 1.0, 0.0).astype(f32)
            step = min(width, part)
            for c in range(0, width, step):
                lane = t * width + c
                out[lane // part, :, lane % part : lane % part + step] = value[:, c : c + step]

    for copy in small:
        copy.wait()

    @pl.when(g == 0)
    def _():
        far[...] = own[...]

    stack(own, own_split)
    def backward(k, carry):
        tile_copy(k).wait()
        products[k] = multiply(own_split[rows[0, k]], k, NN)
        return carry

    lax.fori_loop(0, slots, backward, 0)
    scatter(cols, back)

    pl.semaphore_wait(barrier, greeted)

    lanes = pl.ds(pl.multiple_of(g * part, part), part)
    far_copies = []
    for d in range(groups):
        other = lax.rem(g + d, groups)
        far_copies.append(
            send(
                basis_hbm.at[:, lanes], far.at[:, lanes], far_send.at[d], far_recv.at[d],
                at(other, p - other),
            )
        )
        pl.when(other != 0)(far_copies[d].start)

    plane_copies = []
    for d in range(1, groups):
        h = lax.rem(g + d, groups)
        plane_copies.append(
            send(back.at[h], plane.at[d - 1], plane_send.at[d], plane_recv.at[d], at(h, p))
        )
    for copy in plane_copies:
        copy.start()

    back_copies = []
    for d in range(groups):
        diagonal = lax.rem(g - d + groups, groups)
        held = plane.at[d - 1] if d else back.at[g]
        back_copies.append(
            (
                diagonal != 0, held,
                send(held, arrived.at[d], back_send.at[d], back_recv.at[d], at(g, p + diagonal)),
            )
        )

    def passed_on(d):
        remote, held, copy = back_copies[d]
        pl.when(remote)(copy.start)

        @pl.when(jnp.logical_not(remote))
        def _():
            arrived[d] = held[...]

    passed_on(0)

    both[0:vectors] = own[...]
    both[vectors:] = prev[...]
    pair_slot, chip = lax.rem(p, 2), p // 2
    pair[pair_slot, :, : 4 * vectors] = packed(exact(own[...], both[...], NT))
    offset[...] = energies[...] * own[...] - exact(beta_prev[...], prev[...], NN)

    for d in range(1, groups):
        plane_copies[d - 1].wait_recv()
        passed_on(d)

    @pl.when(g != 0)
    def _():
        for copy in far_copies:
            copy.wait_recv()

    stack(far, far_split)

    def forward(k, carry):
        products[k] = multiply(far_split[cols[0, k]], k, NT)
        return carry

    lax.fori_loop(0, slots, forward, 0)
    scatter(rows, forth)

    forth_copies = []
    for d in range(1, groups):
        h = lax.rem(g + d, groups)
        forth_copies.append(
            send(forth.at[h], arrived.at[groups + d - 1], forth_send.at[d], forth_recv.at[d], at(h, p))
        )
    for copy in forth_copies:
        copy.start()
    for remote, held, copy in back_copies:
        pl.when(remote)(copy.wait_recv)
    for copy in forth_copies:
        copy.wait_recv()

    mine = forth[g]
    for d in range(2 * groups - 1):
        mine = mine + arrived[d]
    gathered[g] = mine

    gather_copies = [
        send(gathered.at[g], gathered.at[g], gather_send.at[d], gather_recv.at[d], at(g + d, p))
        for d in range(1, groups)
    ]
    for copy in gather_copies:
        copy.start()
    for copy in gather_copies:
        copy.wait_recv()

    for h in range(groups):
        lanes = slice(h * part, (h + 1) * part)
        both[vectors:, lanes] = gathered[h] + offset[:, lanes]
    pair[pair_slot, :, 4 * vectors :] = packed(exact(both[vectors:], both[...], NT))

    pair_copy = send(
        pair.at[pair_slot], pair.at[pair_slot], pair_sem.at[0], pair_sem.at[1],
        at(g, p + 1 - 2 * pair_slot),
    )
    pair_copy.start()
    rest_copy = pltpu.make_async_copy(both.at[vectors:], rest_hbm, in_sem.at[0])
    rest_copy.start()
    pair_copy.wait_recv()
    late[chip] = pair[0] + pair[1]
    late_copies = [
        send(late.at[chip], late.at[chip], late_send.at[d], late_recv.at[d], at(g, p + 2 * d))
        for d in range(1, segs // 2)
    ]
    for copy in late_copies:
        copy.start()
    for copy in plane_copies + forth_copies + gather_copies + [pair_copy]:
        copy.wait_send()
    for remote, held, copy in back_copies:
        pl.when(remote)(copy.wait_send)
    for d in range(groups):
        pl.when(lax.rem(g + d, groups) != 0)(far_copies[d].wait_send)
    for copy in late_copies:
        copy.wait()
    after = late[0]
    for s in range(1, segs // 2):
        after = after + late[s]
    sums_ref[...] = after
    rest_copy.wait()


def finish(
    total, rest_hbm, basis_hbm, sums_ref, beta_prev_ref, next_ref, alpha_ref, beta_ref, rest, basis, sem
):
    copies = [
        pltpu.make_async_copy(rest_hbm, rest, sem.at[0]),
        pltpu.make_async_copy(basis_hbm, basis, sem.at[1]),
    ]
    for copy in copies:
        copy.start()
    vectors = beta_prev_ref.shape[0]
    before = unpacked(sums_ref[:, : 4 * vectors])
    after = unpacked(sums_ref[:, 4 * vectors :])
    basis_basis, basis_prev = before[:, :vectors], before[:, vectors:]
    rest_basis, rest_rest = after[:, :vectors], after[:, vectors:]
    alpha_t = (rest_basis + exact(beta_prev_ref[...], basis_prev, NT)) / total
    alpha_ref[...] = alpha_t.T
    gram = (
        rest_rest
        + exact(exact(alpha_t, basis_basis, NN) - rest_basis, alpha_t, NT)
        - exact(alpha_t, rest_basis, NT)
    ) / total
    upper, inverse = factored(gram)
    beta_ref[...] = upper.T
    for copy in copies:
        copy.wait()
    residual = rest[...] - exact(alpha_t, basis[...], NN)
    next_ref[...] = exact(inverse, residual, NN)


def shards(groups, segs, tiles, tile_row, tile_col, tile_count, energies, basis, prev_basis, beta_prev):
    slots, width = tiles.shape[2], tiles.shape[-1]
    vectors, length = basis.shape
    sides, part = length // width, length // groups
    dma = pltpu.SemaphoreType.DMA
    block = (vectors, length)
    vmem = pl.BlockSpec(memory_space=pltpu.VMEM)
    rest, sums = pl.pallas_call(
        functools.partial(kernel, groups, segs),
        out_shape=(
            jax.ShapeDtypeStruct(block, f32),
            jax.ShapeDtypeStruct((vectors // 2, 8 * vectors), f32),
        ),
        in_specs=[pl.BlockSpec(memory_space=pltpu.HBM)] * 8,
        out_specs=(pl.BlockSpec(memory_space=pltpu.HBM), vmem),
        scratch_shapes=[
            pltpu.VMEM((slots, width, width), f32),
            pltpu.SMEM((1, slots), jnp.int32),
            pltpu.SMEM((1, slots), jnp.int32),
            pltpu.SMEM((1, 1), jnp.int32),
            pltpu.VMEM((1, length), f32),
            pltpu.VMEM(block, f32),
            pltpu.VMEM(block, f32),
            pltpu.VMEM(block, f32),
            pltpu.VMEM((vectors, vectors), f32),
            pltpu.VMEM((sides, 2 * vectors, width), bf16),
            pltpu.VMEM((sides, 2 * vectors, width), bf16),
            pltpu.VMEM((slots, vectors, width), f32),
            pltpu.VMEM((groups, vectors, part), f32),
            pltpu.VMEM((groups - 1, vectors, part), f32),
            pltpu.VMEM((groups, vectors, part), f32),
            pltpu.VMEM((2 * groups - 1, vectors, part), f32),
            pltpu.VMEM((groups, vectors, part), f32),
            pltpu.VMEM(block, f32),
            pltpu.VMEM((2 * vectors, length), f32),
            pltpu.VMEM((2, vectors // 2, 8 * vectors), f32),
            pltpu.VMEM((segs // 2, vectors // 2, 8 * vectors), f32),
            dma((7,)), dma((slots,)), dma((groups,)), dma((groups,)),
            dma((groups,)), dma((groups,)), dma((groups,)), dma((groups,)),
            dma((groups,)), dma((groups,)), dma((groups,)), dma((groups,)),
            dma((2,)), dma((segs // 2,)), dma((segs // 2,)),
        ],
        compiler_params=pltpu.CompilerParams(collective_id=0, has_side_effects=True),
    )(
        tiles.reshape(slots, width, width),
        tile_row.reshape(1, slots),
        tile_col.reshape(1, slots),
        tile_count.reshape(1, 1),
        energies.reshape(1, length),
        basis,
        prev_basis,
        beta_prev,
    )
    return pl.pallas_call(
        functools.partial(finish, float(length * segs)),
        out_shape=(
            jax.ShapeDtypeStruct(block, f32),
            jax.ShapeDtypeStruct((vectors, vectors), f32),
            jax.ShapeDtypeStruct((vectors, vectors), f32),
        ),
        in_specs=[pl.BlockSpec(memory_space=pltpu.HBM)] * 2 + [vmem] * 2,
        out_specs=(vmem, vmem, vmem),
        scratch_shapes=[pltpu.VMEM(block, f32), pltpu.VMEM(block, f32), dma((2,))],
    )(rest, basis, sums, beta_prev)


def solution(mesh):
    groups, segs = mesh.shape["grp"], mesh.shape["pos"]
    in_specs = (
        P("grp", "pos", None, None, None),
        P("grp", "pos", None),
        P("grp", "pos", None),
        P("grp", "pos"),
        P("pos"),
        P(None, "pos"),
        P(None, "pos"),
        P(),
    )
    out_specs = (P(None, "pos"), P(), P())
    return jax.shard_map(
        functools.partial(shards, groups, segs),
        mesh=mesh, in_specs=in_specs, out_specs=out_specs, check_vma=False,
    )
```

```python
import functools

import jax
import jax.numpy as jnp
from jax import lax
from jax.experimental import pallas as pl
from jax.experimental.pallas import tpu as pltpu
from jax.sharding import PartitionSpec as P

MESH = pl.DeviceIdType.MESH
NT = (((1,), (1,)), ((), ()))
NN = (((1,), (0,)), ((), ()))
f32 = jnp.float32
bf16 = jnp.bfloat16


def exact(left, right, dims):
    return lax.dot_general(
        left, right, dims, precision=lax.Precision.HIGHEST, preferred_element_type=f32
    )


def split(values):
    high = values.astype(bf16)
    return high, (values - high.astype(f32)).astype(bf16)


def packed(values):
    half = values.shape[0] // 2
    return jnp.concatenate([values[:half], values[half:]], axis=1)


def unpacked(values):
    half = values.shape[1] // 2
    return jnp.concatenate([values[:, :half], values[:, half:]], axis=0)


def factored(gram):
    n = gram.shape[0]
    wide = jnp.concatenate([gram, jnp.eye(n, dtype=f32)], axis=1)
    row_at = lax.broadcasted_iota(jnp.int32, (n, 1), 0)
    columns = [jnp.broadcast_to(gram[:, k : k + 1], (n, 2 * n)) for k in range(n)]
    done = jnp.zeros((n, 2 * n), f32)
    for j in range(n):
        corner = columns[j][j : j + 1]
        inverse = 1.0 / corner
        row = wide[j : j + 1]
        done = jnp.where(row_at == j, row * lax.rsqrt(corner), done)
        for k in range(j + 1, n):
            columns[k] = columns[k] - columns[j] * (columns[k][j : j + 1] * inverse)
        wide = wide - columns[j] * (row * inverse)
    return done[:, :n], done[:, n:]


def kernel(
    groups, segs,
    tiles_hbm, row_hbm, col_hbm, count_hbm, energies_hbm, basis_hbm, prev_hbm, beta_prev_hbm,
    rest_hbm, sums_ref,
    tiles, rows, cols, count, energies, own, far, prev, beta_prev,
    own_split, far_split, products, back, forth, arrived, gathered, offset, both, pair, late,
    in_sem, tile_sem, far_send, far_recv, back_send, back_recv, forth_send, forth_recv,
    gather_send, gather_recv, pair_sem, late_send, late_recv,
):
    g, p = lax.axis_index("grp"), lax.axis_index("pos")
    slots, width = tiles.shape[0], tiles.shape[-1]
    vectors, length = own.shape
    sides = length // width
    part = length // groups

    def at(group, pos):
        return (lax.rem(group + groups, groups), lax.rem(pos + segs, segs))

    def send(src, dst, send_sem, recv_sem, to):
        return pltpu.make_async_remote_copy(
            src_ref=src, dst_ref=dst, send_sem=send_sem, recv_sem=recv_sem,
            device_id=to, device_id_type=MESH,
        )

    barrier = pltpu.get_barrier_semaphore()
    greeted = 0
    for d in range(1, segs):
        pl.semaphore_signal(barrier, inc=1, device_id=at(g, p + d), device_id_type=MESH)
        greeted += 1
    for d in range(1, groups):
        pl.semaphore_signal(barrier, inc=1, device_id=at(g + d, p), device_id_type=MESH)
        source = lax.rem(g - d + groups, groups)
        pl.semaphore_signal(barrier, inc=1, device_id=at(source, p - source), device_id_type=MESH)
        pl.semaphore_signal(barrier, inc=1, device_id=at(g + d, p + g), device_id_type=MESH)
        greeted += 3

    small = [
        pltpu.make_async_copy(src, dst, in_sem.at[i])
        for i, (src, dst) in enumerate([
            (basis_hbm, own), (prev_hbm, prev), (energies_hbm, energies),
            (beta_prev_hbm, beta_prev), (row_hbm, rows), (col_hbm, cols), (count_hbm, count),
        ])
    ]
    for copy in small:
        copy.start()

    def tile_copy(k):
        return pltpu.make_async_copy(tiles_hbm.at[k], tiles.at[k], tile_sem.at[k])

    for k in range(slots):
        tile_copy(k).start()

    def stack(ref, out):
        for t in range(sides):
            high, low = split(ref[:, t * width : (t + 1) * width])
            out[t] = jnp.concatenate([high, low], axis=0)

    def multiply(picked, k, dims):
        high, low = split(tiles[k])
        both_parts = lax.dot_general(picked, high, dims, preferred_element_type=f32)
        both_parts += lax.dot_general(picked, low, dims, preferred_element_type=f32)
        return both_parts[:vectors] + both_parts[vectors:]

    def scatter(index, out):
        for t in range(sides):
            value = jnp.zeros((vectors, width), f32)
            for k in range(slots):
                live = jnp.logical_and(index[0, k] == t, k < count[0, 0])
                value = value + products[k] * jnp.where(live, 1.0, 0.0).astype(f32)
            step = min(width, part)
            for c in range(0, width, step):
                lane = t * width + c
                out[lane // part, :, lane % part : lane % part + step] = value[:, c : c + step]

    pl.semaphore_wait(barrier, greeted)

    lanes = pl.ds(pl.multiple_of(g * part, part), part)
    far_copies = []
    for d in range(groups):
        other = lax.rem(g + d, groups)
        far_copies.append(
            send(
                basis_hbm.at[:, lanes], far.at[:, lanes], far_send.at[d], far_recv.at[d],
                at(other, p - other),
            )
        )
        pl.when(other != 0)(far_copies[d].start)

    for copy in small:
        copy.wait()

    @pl.when(g == 0)
    def _():
        far[...] = own[...]

    stack(own, own_split)
    def backward(k, carry):
        tile_copy(k).wait()
        products[k] = multiply(own_split[rows[0, k]], k, NN)
        return carry

    lax.fori_loop(0, slots, backward, 0)
    scatter(cols, back)

    back_copies = []
    for d in range(groups):
        h = lax.rem(g + d, groups)
        back_copies.append(
            send(back.at[h], arrived.at[d], back_send.at[d], back_recv.at[d], at(h, p + g))
        )
    for copy in back_copies[1:]:
        copy.start()

    @pl.when(g != 0)
    def _():
        back_copies[0].start()

    @pl.when(g == 0)
    def _():
        arrived[0] = back[g]

    both[0:vectors] = own[...]
    both[vectors:] = prev[...]
    pair_slot, chip = lax.rem(p, 2), p // 2
    pair[pair_slot, :, : 4 * vectors] = packed(exact(own[...], both[...], NT))
    offset[...] = energies[...] * own[...] - exact(beta_prev[...], prev[...], NN)

    @pl.when(g != 0)
    def _():
        for copy in far_copies:
            copy.wait_recv()

    stack(far, far_split)

    def forward(k, carry):
        products[k] = multiply(far_split[cols[0, k]], k, NT)
        return carry

    lax.fori_loop(0, slots, forward, 0)
    scatter(rows, forth)

    forth_copies = []
    for d in range(1, groups):
        h = lax.rem(g + d, groups)
        forth_copies.append(
            send(forth.at[h], arrived.at[groups + d - 1], forth_send.at[d], forth_recv.at[d], at(h, p))
        )
    for copy in forth_copies:
        copy.start()
    for copy in forth_copies + back_copies[1:]:
        copy.wait_recv()

    pl.when(g != 0)(back_copies[0].wait_recv)

    mine = forth[g]
    for d in range(2 * groups - 1):
        mine = mine + arrived[d]
    gathered[g] = mine

    gather_copies = [
        send(gathered.at[g], gathered.at[g], gather_send.at[d], gather_recv.at[d], at(g + d, p))
        for d in range(1, groups)
    ]
    for copy in gather_copies:
        copy.start()
    for copy in gather_copies:
        copy.wait_recv()

    for h in range(groups):
        lanes = slice(h * part, (h + 1) * part)
        both[vectors:, lanes] = gathered[h] + offset[:, lanes]
    pair[pair_slot, :, 4 * vectors :] = packed(exact(both[vectors:], both[...], NT))

    pair_copy = send(
        pair.at[pair_slot], pair.at[pair_slot], pair_sem.at[0], pair_sem.at[1],
        at(g, p + 1 - 2 * pair_slot),
    )
    pair_copy.start()
    rest_copy = pltpu.make_async_copy(both.at[vectors:], rest_hbm, in_sem.at[0])
    rest_copy.start()
    pair_copy.wait_recv()
    late[chip] = pair[0] + pair[1]
    late_copies = [
        send(late.at[chip], late.at[chip], late_send.at[d], late_recv.at[d], at(g, p + 2 * d))
        for d in range(1, segs // 2)
    ]
    for copy in late_copies:
        copy.start()
    for copy in forth_copies + back_copies[1:] + gather_copies + [pair_copy]:
        copy.wait_send()
    pl.when(g != 0)(back_copies[0].wait_send)
    for d in range(groups):
        pl.when(lax.rem(g + d, groups) != 0)(far_copies[d].wait_send)
    for copy in late_copies:
        copy.wait()
    after = late[0]
    for s in range(1, segs // 2):
        after = after + late[s]
    sums_ref[...] = after
    rest_copy.wait()


def finish(
    total, rest_hbm, basis_hbm, sums_ref, beta_prev_ref, next_ref, alpha_ref, beta_ref, rest, basis, sem
):
    copies = [
        pltpu.make_async_copy(rest_hbm, rest, sem.at[0]),
        pltpu.make_async_copy(basis_hbm, basis, sem.at[1]),
    ]
    for copy in copies:
        copy.start()
    vectors = beta_prev_ref.shape[0]
    before = unpacked(sums_ref[:, : 4 * vectors])
    after = unpacked(sums_ref[:, 4 * vectors :])
    basis_basis, basis_prev = before[:, :vectors], before[:, vectors:]
    rest_basis, rest_rest = after[:, :vectors], after[:, vectors:]
    alpha_t = (rest_basis + exact(beta_prev_ref[...], basis_prev, NT)) / total
    alpha_ref[...] = alpha_t.T
    gram = (
        rest_rest
        + exact(exact(alpha_t, basis_basis, NN) - rest_basis, alpha_t, NT)
        - exact(alpha_t, rest_basis, NT)
    ) / total
    upper, inverse = factored(gram)
    beta_ref[...] = upper.T
    for copy in copies:
        copy.wait()
    residual = rest[...] - exact(alpha_t, basis[...], NN)
    next_ref[...] = exact(inverse, residual, NN)


def shards(groups, segs, tiles, tile_row, tile_col, tile_count, energies, basis, prev_basis, beta_prev):
    slots, width = tiles.shape[2], tiles.shape[-1]
    vectors, length = basis.shape
    sides, part = length // width, length // groups
    dma = pltpu.SemaphoreType.DMA
    block = (vectors, length)
    vmem = pl.BlockSpec(memory_space=pltpu.VMEM)
    rest, sums = pl.pallas_call(
        functools.partial(kernel, groups, segs),
        out_shape=(
            jax.ShapeDtypeStruct(block, f32),
            jax.ShapeDtypeStruct((vectors // 2, 8 * vectors), f32),
        ),
        in_specs=[pl.BlockSpec(memory_space=pltpu.HBM)] * 8,
        out_specs=(pl.BlockSpec(memory_space=pltpu.HBM), vmem),
        scratch_shapes=[
            pltpu.VMEM((slots, width, width), f32),
            pltpu.SMEM((1, slots), jnp.int32),
            pltpu.SMEM((1, slots), jnp.int32),
            pltpu.SMEM((1, 1), jnp.int32),
            pltpu.VMEM((1, length), f32),
            pltpu.VMEM(block, f32),
            pltpu.VMEM(block, f32),
            pltpu.VMEM(block, f32),
            pltpu.VMEM((vectors, vectors), f32),
            pltpu.VMEM((sides, 2 * vectors, width), bf16),
            pltpu.VMEM((sides, 2 * vectors, width), bf16),
            pltpu.VMEM((slots, vectors, width), f32),
            pltpu.VMEM((groups, vectors, part), f32),
            pltpu.VMEM((groups, vectors, part), f32),
            pltpu.VMEM((2 * groups - 1, vectors, part), f32),
            pltpu.VMEM((groups, vectors, part), f32),
            pltpu.VMEM(block, f32),
            pltpu.VMEM((2 * vectors, length), f32),
            pltpu.VMEM((2, vectors // 2, 8 * vectors), f32),
            pltpu.VMEM((segs // 2, vectors // 2, 8 * vectors), f32),
            dma((7,)), dma((slots,)), dma((groups,)), dma((groups,)),
            dma((groups,)), dma((groups,)), dma((groups,)), dma((groups,)),
            dma((groups,)), dma((groups,)),
            dma((2,)), dma((segs // 2,)), dma((segs // 2,)),
        ],
        compiler_params=pltpu.CompilerParams(collective_id=0, has_side_effects=True),
    )(
        tiles.reshape(slots, width, width),
        tile_row.reshape(1, slots),
        tile_col.reshape(1, slots),
        tile_count.reshape(1, 1),
        energies.reshape(1, length),
        basis,
        prev_basis,
        beta_prev,
    )
    return pl.pallas_call(
        functools.partial(finish, float(length * segs)),
        out_shape=(
            jax.ShapeDtypeStruct(block, f32),
            jax.ShapeDtypeStruct((vectors, vectors), f32),
            jax.ShapeDtypeStruct((vectors, vectors), f32),
        ),
        in_specs=[pl.BlockSpec(memory_space=pltpu.HBM)] * 2 + [vmem] * 2,
        out_specs=(vmem, vmem, vmem),
        scratch_shapes=[pltpu.VMEM(block, f32), pltpu.VMEM(block, f32), dma((2,))],
    )(rest, basis, sums, beta_prev)


def solution(mesh):
    groups, segs = mesh.shape["grp"], mesh.shape["pos"]
    in_specs = (
        P("grp", "pos", None, None, None),
        P("grp", "pos", None),
        P("grp", "pos", None),
        P("grp", "pos"),
        P("pos"),
        P(None, "pos"),
        P(None, "pos"),
        P(),
    )
    out_specs = (P(None, "pos"), P(), P())
    return jax.shard_map(
        functools.partial(shards, groups, segs),
        mesh=mesh, in_specs=in_specs, out_specs=out_specs, check_vma=False,
    )
```
